32 devices in a mesh: groups: 2 (over y), dp: 8 (over z, x), cuts: 2 (over core).
Axes of the slice: x: 2, y: 2, z: 4, core: 2. Of those that a mesh axis runs over, the one named last changes fastest.
Arguments:
- activations: bfloat16 [768, 7168], P(('groups', 'dp'), 'cuts'), parts along dimension 0, may hold values from -6 to 6
- out_grads: bfloat16 [768, 4096], P(('groups', 'dp'), 'cuts'), parts along dimension 0, may hold values from -6 to 6
- counts: int32 [16, 8], P(('groups', 'dp')), parts along dimension 0, may hold values from 1 to 24, 48 in all within a row
- doc_slots: int32 [128], P('groups'), parts along dimension 0, may hold values from 0 to 63, each once
- proj_in: bfloat16 [7168, 64], P('cuts'), may hold values from -0.0625 to 0.0625
- proj_out: bfloat16 [4096, 64], P('cuts'), may hold values from -0.09375 to 0.09375
- queries: bfloat16 [512, 4096], P(None, ('dp', 'cuts')), may hold values from -0.5 to 0.5
Outputs:
- scores: float32 [512, 128], P(('dp', 'cuts'), 'groups'), parts along dimension 1
The draws below stay inside these ranges and needn't reach their ends.
There are 2 independent parts, one for each index of `groups`. The reference program is written for one: setup_inputs(seed, part) draws one part's arguments, and reference() takes and returns one part's arrays. A program takes and returns all parts, laid end to end along the dimension named above; an argument that names none is the same for every part. Nothing has to cross between parts.
Inputs may be any that keep to these rules, and one draw needn't show every extreme that they name: The 8 counts of each dp index sum to 48. `doc_slots`: each document gets a different column.
All inputs are finite; a program needn't handle non-finite values.
Results may differ from the reference program's by a relative error of at most 0.0029.
Values may be sent and summed in bfloat16 or wider, within the bound.
No kernel may reach another device: no remote copies, remote signals or barrier semaphores. Data moves between devices by JAX's collectives and lax.ppermute only.
A program may use at most 64 MiB of HBM per device.

```python
import math
import jax
import jax.numpy as jnp
import numpy as np
from jax import lax

D = 4096
FF = 7168
RANK = 64
QUERIES = 512
ROWS_DEV = 48
DOC_DEV = 8
SRC = 8
DOCS = 64
ROWS = 384
ENTRIES = 4096


def block_levels(own_key, extent, pieces, smallest, largest):
    loudness, own = 1.0, jax.random.fold_in(own_key, 6)
    for dim, shards_of in pieces:
        heights = jnp.exp(jax.random.uniform(jax.random.fold_in(own, dim), (shards_of,), jnp.float32, smallest / len(pieces), largest / len(pieces)))
        loudness = loudness * jnp.repeat(heights, extent[dim] // shards_of).reshape([-1 if axis == dim else 1 for axis in range(len(extent))])
    return loudness


def profile(amount, total, bound, skew):
    portions = [(1 << 20) // math.isqrt(rank ** skew) + 1 for rank in range(2, amount + 1)]
    surplus, given = total - bound - (amount - 1), [1] * (amount - 1)
    while surplus > 0:
        candidates = [i for i in range(amount - 1) if given[i] < bound]
        pool, left = sum([portions[i] for i in candidates]), surplus
        for i in candidates:
            addition = min(bound - given[i], max(1, left * portions[i] // pool), surplus)
            given[i] = given[i] + addition
            surplus = surplus - addition
    return np.array([bound] + given)


def ragged_sizes(rng, count, total, reach, lean):
    if count == 2:
        one = jax.random.randint(rng, (), max(1, total - reach), min(reach, total - 1) + 1)
        return jnp.stack([one, total - one])
    tallies = jnp.asarray(profile(count, total, reach, lean), jnp.int32)
    couples = (count - 1) // 2
    source_of, sink = tallies[1:1 + 2 * couples:2], tallies[2:2 + 2 * couples:2]
    slack = jnp.minimum(source_of - 1, reach - sink)
    shifted = jax.random.randint(jax.random.fold_in(rng, 1), (couples,), 0, 1 << 20) % (slack + 1)
    tallies = tallies.at[1:1 + 2 * couples:2].set(source_of - shifted).at[2:2 + 2 * couples:2].set(sink + shifted)
    return tallies[jax.random.permutation(jax.random.fold_in(rng, 2), count)]


def normal_values(rng, dims, width, bound, cuts=(), kind=jnp.bfloat16):
    result = jax.random.normal(rng, dims, jnp.float32) * width
    if len(cuts) > 0:
        result = block_levels(rng, dims, cuts, -0.22, 0.18) * result
    return jnp.clip(result, min=-bound, max=bound).astype(kind)


def setup_inputs(seed: int = 0, part: int = 0) -> dict:
    seeds = jax.random.split(jax.random.key(seed), 8)
    own_keys = jax.random.split(jax.random.fold_in(seeds[7], part), 8)
    activations = normal_values(own_keys[0], (ROWS, FF), 1.0, 6.0, ((0, 8), (1, 2)))
    out_grads = normal_values(own_keys[1], (ROWS, D), 1.0, 6.0, ((0, 8), (1, 2)))
    counts = jax.vmap(lambda own: ragged_sizes(own, DOC_DEV, ROWS_DEV, ROWS_DEV // 2, 2))(jax.random.split(own_keys[2], SRC)).reshape((SRC, DOC_DEV)).astype(jnp.int32)
    doc_slots = jax.random.permutation(own_keys[3], DOCS).astype(jnp.int32)
    proj_in = normal_values(seeds[4], (FF, RANK), FF ** -0.5, 0.0625, ((0, 2),))
    proj_out = normal_values(seeds[5], (D, RANK), D ** -0.5, 0.09375, ((0, 2),))
    queries = normal_values(seeds[6], (QUERIES, ENTRIES), 0.0625, 0.5, ((1, 16),))
    return dict(activations=activations, out_grads=out_grads, counts=counts, doc_slots=doc_slots, proj_in=proj_in, proj_out=proj_out, queries=queries)


def reference(activations, out_grads, counts, doc_slots, proj_in, proj_out, queries):
    def one_source(packed):
        acts_rows, grad_rows, doc_counts = packed
        inward = jnp.dot(acts_rows, proj_in, preferred_element_type=jnp.float32)
        outward = jnp.dot(grad_rows, proj_out, preferred_element_type=jnp.float32)
        ending = jnp.cumsum(doc_counts).astype(jnp.int32)
        position = lax.iota(jnp.int32, ROWS_DEV)
        owner_doc = jnp.sum((ending[None, :] <= position[:, None]).astype(jnp.int32), axis=1)
        member = (owner_doc[:, None] == lax.iota(jnp.int32, DOC_DEV)[None, :]).astype(jnp.float32)
        weights = member / doc_counts.astype(jnp.float32)[None, :]
        gradient = jnp.einsum("td,tr,ti->dri", weights, outward, inward, precision=lax.Precision.HIGHEST)
        return gradient.reshape(DOC_DEV, RANK * RANK)

    per_source = lax.map(one_source, (activations.reshape(SRC, ROWS_DEV, FF), out_grads.reshape(SRC, ROWS_DEV, D), counts))
    gradients = per_source.reshape(DOCS, RANK * RANK).astype(jnp.bfloat16)
    source_scores = lax.dot_general(queries, gradients, (((1,), (1,)), ((), ())), preferred_element_type=jnp.float32)
    inverse = jnp.argsort(doc_slots).astype(jnp.int32)
    return jnp.take(source_scores, inverse, axis=1)
```

```python
import jax
import jax.numpy as jnp
from jax import lax
from jax.experimental import pallas as pl
from jax.experimental.pallas import tpu as pltpu
from jax.sharding import PartitionSpec as P

TILE = 8


def score_kernel(row_count, rank, payload_ref, query_ref, scores_ref):
    sources = payload_ref.shape[0]
    split = query_ref.shape[1] // rank
    query_rows = scores_ref.shape[0]
    chunks = query_ref.shape[0] // query_rows
    columns = scores_ref.shape[1]
    tokens = sources * row_count
    payload = payload_ref[...]
    turned = payload[:, :row_count, :].reshape(tokens, 2 * rank).T
    inward, outward = turned[:rank], turned[rank:]
    high = inward.astype(jnp.bfloat16)
    low = (inward - high.astype(jnp.float32)).astype(jnp.bfloat16)
    query = query_ref[...]
    query = jnp.concatenate([query, query], axis=1)
    blank = jnp.zeros_like(high)
    total = jnp.zeros((query_rows, tokens), jnp.float32)
    for part in range(split):
        column = [blank] * (2 * split)
        column[part], column[split + part] = high, low
        met = jnp.dot(query, jnp.concatenate(column, axis=0), preferred_element_type=jnp.float32)
        for chunk in range(chunks):
            entry = chunk * split + part
            total = total + met[chunk * query_rows:(chunk + 1) * query_rows] * outward[entry:entry + 1]
    marks = payload[:, row_count:, :].reshape(sources * TILE, 2 * rank).T
    slots = jnp.concatenate([marks[:row_count, s * TILE:s * TILE + 1] for s in range(sources)], axis=0)
    column_of = lax.broadcasted_iota(jnp.int32, (tokens, columns), 1)
    member = (slots.astype(jnp.int32) == column_of).astype(jnp.bfloat16)
    total_high = total.astype(jnp.bfloat16)
    total_low = (total - total_high.astype(jnp.float32)).astype(jnp.bfloat16)
    scores = jnp.dot(total_high, member, preferred_element_type=jnp.float32)
    scores = scores + jnp.dot(total_low, member, preferred_element_type=jnp.float32)

    @pl.when(pl.program_id(0) == 0)
    def _():
        scores_ref[...] = scores

    @pl.when(pl.program_id(0) > 0)
    def _():
        scores_ref[...] += scores


def score(payload, query, query_rows, columns, row_count, rank):
    sources = payload.shape[0]
    step = min(sources, 8)
    return pl.pallas_call(
        lambda *refs: score_kernel(row_count, rank, *refs),
        grid=(sources // step,),
        in_specs=[
            pl.BlockSpec((step,) + payload.shape[1:], lambda i: (i, 0, 0)),
            pl.BlockSpec(query.shape, lambda i: (0, 0)),
        ],
        out_specs=pl.BlockSpec((query_rows, columns), lambda i: (0, 0)),
        out_shape=jax.ShapeDtypeStruct((query_rows, columns), jnp.float32),
        compiler_params=pltpu.CompilerParams(vmem_limit_bytes=48 * 1024 * 1024),
        name="score",
    )(payload, query)


def exchange(value, axis, bit):
    count = lax.axis_size(axis)
    return lax.ppermute(value, axis, [(i, i ^ bit) for i in range(count)])


def on_device(activations, out_grads, counts, doc_slots, proj_in, proj_out, queries):
    row_count = activations.shape[0]
    rank = proj_in.shape[1]
    doc_count = counts.shape[1]
    cut_count = lax.axis_size("cuts")
    data_count = lax.axis_size("dp")
    parts = cut_count * data_count
    query_rows = queries.shape[0] // parts
    width = queries.shape[1]

    arrived = lax.all_to_all(queries, ("dp", "cuts"), split_axis=0, concat_axis=0, tiled=True)
    if width % rank:
        arrived = arrived.reshape(parts, query_rows, width).transpose(1, 0, 2)
        arrived = arrived.reshape(query_rows, -1, rank).transpose(1, 0, 2).reshape(-1, rank)

    inward = jnp.dot(activations, proj_in, preferred_element_type=jnp.float32)
    outward = jnp.dot(out_grads, proj_out, preferred_element_type=jnp.float32)
    tally = counts[0]
    order = lax.iota(jnp.int32, doc_count)
    ending = jnp.sum(jnp.where(order[None, :] <= order[:, None], tally[None, :], 0), axis=1)
    starting = ending - tally
    position = lax.iota(jnp.int32, row_count)
    member = (starting[None, :] <= position[:, None]) & (position[:, None] < ending[None, :])
    inverse = jnp.sum(jnp.where(member, 1.0 / tally.astype(jnp.float32)[None, :], 0.0), axis=1)
    own_slots = lax.dynamic_slice_in_dim(doc_slots, lax.axis_index("dp") * doc_count, doc_count)
    slots = jnp.sum(jnp.where(member, own_slots[None, :], 0), axis=1).astype(jnp.float32)
    both = jnp.concatenate([inward, outward * inverse[:, None]], axis=1)
    bit = 1
    while bit < cut_count:
        both = both + exchange(both, "cuts", bit)
        bit *= 2
    marks = jnp.zeros((TILE, 2 * rank), jnp.float32).at[0, :row_count].set(slots)
    payload = jnp.concatenate([both, marks], axis=0)[None]
    bit = 1
    while bit < data_count:
        payload = jnp.concatenate([payload, exchange(payload, "dp", bit)], axis=0)
        bit *= 2
    return score(payload, arrived, query_rows, doc_slots.shape[0], row_count, rank)


def solution(mesh):
    placed = (
        P(("groups", "dp"), "cuts"),
        P(("groups", "dp"), "cuts"),
        P(("groups", "dp"), None),
        P("groups"),
        P("cuts", None),
        P("cuts", None),
        P(None, ("dp", "cuts")),
    )
    return jax.shard_map(
        on_device,
        mesh=mesh,
        in_specs=placed,
        out_specs=P(("dp", "cuts"), "groups"),
        check_vma=False,
    )
```

```python
import functools
import math

import jax
import jax.numpy as jnp
from jax import lax
from jax.experimental import pallas as pl
from jax.experimental.pallas import tpu as pltpu
from jax.sharding import PartitionSpec as P

TILE = 8
LANES = 128


def project_kernel(*refs):
    sources, payload_ref, held, sem = refs[:6], refs[6], refs[7:13], refs[13]
    copies = [pltpu.make_async_copy(source, kept, sem.at[i]) for i, (source, kept) in enumerate(zip(sources, held))]
    for copy in copies:
        copy.start()
    acts_ref, in_ref, grads_ref, out_ref, counts_ref, slots_ref = held
    row_count = acts_ref.shape[0]
    rank = in_ref.shape[0]
    doc_count = counts_ref.shape[1]
    contract = (((1,), (1,)), ((), ()))
    row = lax.broadcasted_iota(jnp.int32, (row_count, rank), 0)
    lane = lax.broadcasted_iota(jnp.int32, (TILE, 2 * rank), 1)
    tally = jnp.ones((row_count, rank), jnp.int32)
    slots = jnp.zeros((TILE, 2 * rank), jnp.int32)
    first_doc = lax.axis_index("dp") * doc_count
    copies[4].wait()
    copies[5].wait()
    start = jnp.int32(0)
    for doc in range(doc_count):
        count = counts_ref[0, doc]
        tally = jnp.where((row >= start) & (row < start + count), count, tally)
        slots = jnp.where((lane >= start) & (lane < start + count), slots_ref[first_doc + doc], slots)
        start = start + count
    leader = (lax.axis_index("cuts") == 0).astype(jnp.float32)
    payload_ref[row_count:, :] = slots.astype(jnp.float32) * leader
    copies[0].wait()
    copies[1].wait()
    inward = lax.dot_general(acts_ref[...], in_ref[...], contract, preferred_element_type=jnp.float32)
    payload_ref[:row_count, :rank] = inward
    copies[2].wait()
    copies[3].wait()
    outward = lax.dot_general(grads_ref[...], out_ref[...], contract, preferred_element_type=jnp.float32)
    payload_ref[:row_count, rank:] = outward / tally.astype(jnp.float32)


def project(counts, doc_slots, activations, out_grads, proj_in, proj_out):
    row_count, rank = activations.shape[0], proj_in.shape[1]
    operands = (activations, proj_in.T, out_grads, proj_out.T, counts, doc_slots)
    spaces = [pltpu.VMEM] * 4 + [pltpu.SMEM] * 2
    return pl.pallas_call(
        project_kernel,
        in_specs=[pl.BlockSpec(memory_space=pltpu.HBM)] * len(operands),
        out_specs=pl.BlockSpec(memory_space=pltpu.VMEM),
        scratch_shapes=[space(operand.shape, operand.dtype) for space, operand in zip(spaces, operands)]
        + [pltpu.SemaphoreType.DMA((len(operands),))],
        out_shape=jax.ShapeDtypeStruct((row_count + TILE, 2 * rank), jnp.float32),
        compiler_params=pltpu.CompilerParams(vmem_limit_bytes=60 * 1024 * 1024),
        name="project",
    )(*operands)


def score_kernel(row_count, rank, origins, other, payload_ref, query_ref, scores_ref, outward_ref):
    sources = payload_ref.shape[0]
    query_rows, columns = scores_ref.shape
    chunks, halves = query_ref.shape[:2]
    split = query_ref.shape[3] // rank
    tokens = sources * row_count
    here = lax.axis_index("dp") * lax.axis_size("cuts") + lax.axis_index("cuts")
    parts = lax.axis_size("dp") * lax.axis_size("cuts")
    half = here // (parts // halves)
    target = halves - 1 - half if other else half
    payload = payload_ref[...]
    turned = payload[:, :row_count, :].reshape(tokens, 2 * rank).T
    inward = turned[:rank]
    outward_ref[...] = turned[rank:]
    high = inward.astype(jnp.bfloat16)
    low = (inward - high.astype(jnp.float32)).astype(jnp.bfloat16)
    blank = jnp.zeros_like(high)
    group = math.gcd(split, max(1, LANES // rank))
    total = jnp.zeros((query_rows, tokens), jnp.float32)
    for part in range(split):
        first = part // group * group
        query = query_ref[:, target, :, first * rank:(first + group) * rank].reshape(chunks * query_rows, group * rank)
        column = [blank] * (2 * group)
        column[part - first], column[part - first + group] = high, low
        met = jnp.dot(
            jnp.concatenate([query, query], axis=1),
            jnp.concatenate(column, axis=0),
            preferred_element_type=jnp.float32,
        )
        for chunk in range(chunks):
            origin = half * chunks + chunk if origins is None else here ^ origins[chunk]
            factor = outward_ref[pl.ds(origin * split + part, 1), :]
            total = total + met[chunk * query_rows:(chunk + 1) * query_rows] * factor
    marks = payload[:, row_count:, :].reshape(sources * TILE, 2 * rank).T
    slots = jnp.concatenate([marks[:row_count, s * TILE:s * TILE + 1] for s in range(sources)], axis=0)
    column_of = lax.broadcasted_iota(jnp.int32, (tokens, columns), 1)
    member = (slots.astype(jnp.int32) == column_of).astype(jnp.bfloat16)
    total_high = total.astype(jnp.bfloat16)
    total_low = (total - total_high.astype(jnp.float32)).astype(jnp.bfloat16)
    scores = jnp.dot(total_high, member, preferred_element_type=jnp.float32)
    scores = scores + jnp.dot(total_low, member, preferred_element_type=jnp.float32)

    @pl.when(pl.program_id(0) == 0)
    def _():
        scores_ref[...] = scores

    @pl.when(pl.program_id(0) > 0)
    def _():
        scores_ref[...] += scores


def score(payload, query, columns, row_count, rank, origins, other):
    sources = payload.shape[0]
    query_rows = query.shape[2]
    step = min(sources, 8)
    return pl.pallas_call(
        functools.partial(score_kernel, row_count, rank, origins, other),
        grid=(sources // step,),
        in_specs=[
            pl.BlockSpec((step,) + payload.shape[1:], lambda i: (i, 0, 0)),
            pl.BlockSpec(query.shape, lambda i: (0, 0, 0, 0)),
        ],
        out_specs=pl.BlockSpec((query_rows, columns), lambda i: (0, 0)),
        out_shape=jax.ShapeDtypeStruct((query_rows, columns), jnp.float32),
        scratch_shapes=[pltpu.VMEM((rank, step * row_count), jnp.float32)],
        compiler_params=pltpu.CompilerParams(vmem_limit_bytes=48 * 1024 * 1024),
        name="score_other" if other else "score_own",
    )(payload, query)


def exchange(value, axis, bit):
    count = lax.axis_size(axis)
    return lax.ppermute(value, axis, [(i, i ^ bit) for i in range(count)])


def on_device(activations, out_grads, counts, doc_slots, proj_in, proj_out, queries):
    row_count = activations.shape[0]
    rank = proj_in.shape[1]
    both = ("dp", "cuts")
    cut_count = lax.axis_size("cuts")
    data_count = lax.axis_size("dp")
    parts = cut_count * data_count
    query_rows = queries.shape[0] // parts
    width = queries.shape[1]

    here = lax.axis_index(both)
    arrived = queries.reshape(1, 2, parts // 2, query_rows, width)
    origins = [0]
    steps = []
    bit = parts // 4
    while bit > 0:
        sides = arrived.reshape(arrived.shape[0], 2, 2, bit, query_rows, width)
        side = (here // bit) % 2
        leaving = lax.dynamic_index_in_dim(sides, 1 - side, 2, keepdims=False)
        staying = lax.dynamic_index_in_dim(sides, side, 2, keepdims=False)
        landed = exchange(leaving, both, bit)
        steps.append(landed)
        if width % rank:
            pair = (jnp.where(side == 0, staying, landed), jnp.where(side == 0, landed, staying))
            arrived = jnp.stack(pair, axis=1).reshape((-1,) + staying.shape[1:])
        else:
            arrived = jnp.concatenate([staying, landed], axis=0)
        origins = origins + [origin ^ bit for origin in origins]
        bit //= 2
    arrived = arrived.reshape(parts // 2, 2, query_rows, width)
    if width % rank:
        arrived = arrived.transpose(1, 2, 0, 3).reshape(2, query_rows, -1, rank).transpose(2, 0, 1, 3)
        origins = None

    payload = project(counts, doc_slots, activations, out_grads, proj_in, proj_out)
    bit = 1
    while bit < cut_count:
        payload = payload + exchange(payload, "cuts", bit)
        bit *= 2
    payload = payload[None]
    bit = data_count // 2
    while bit > 0:
        payload = jnp.concatenate([payload, exchange(payload, "dp", bit)], axis=0)
        bit //= 2
    columns = doc_slots.shape[0]
    theirs = score(payload, arrived, columns, row_count, rank, origins, True)
    own = score(payload, arrived, columns, row_count, rank, origins, False)
    return own + exchange(theirs, both, parts // 2)


def solution(mesh):
    placed = (
        P(("groups", "dp"), "cuts"),
        P(("groups", "dp"), "cuts"),
        P(("groups", "dp"), None),
        P("groups"),
        P("cuts", None),
        P("cuts", None),
        P(None, ("dp", "cuts")),
    )
    return jax.shard_map(
        on_device,
        mesh=mesh,
        in_specs=placed,
        out_specs=P(("dp", "cuts"), "groups"),
        check_vma=False,
    )
```

```python
import functools
import math

import jax
import jax.numpy as jnp
from jax import lax
from jax.experimental import pallas as pl
from jax.experimental.pallas import tpu as pltpu
from jax.sharding import PartitionSpec as P

TILE = 8
LANES = 128


def project_kernel(*refs):
    sources, payload_ref, held, sem = refs[:6], refs[6], refs[7:13], refs[13]
    copies = [pltpu.make_async_copy(source, kept, sem.at[i]) for i, (source, kept) in enumerate(zip(sources, held))]
    for i in (4, 5, 2, 3, 0, 1):
        copies[i].start()
    acts_ref, in_ref, grads_ref, out_ref, counts_ref, slots_ref = held
    row_count = acts_ref.shape[0]
    rank = in_ref.shape[0]
    doc_count = counts_ref.shape[1]
    contract = (((1,), (1,)), ((), ()))
    row = lax.broadcasted_iota(jnp.int32, (row_count, rank), 0)
    lane = lax.broadcasted_iota(jnp.int32, (TILE, 2 * rank), 1)
    tally = jnp.ones((row_count, rank), jnp.int32)
    slots = jnp.zeros((TILE, 2 * rank), jnp.int32)
    first_doc = lax.axis_index("dp") * doc_count
    copies[4].wait()
    copies[5].wait()
    start = jnp.int32(0)
    for doc in range(doc_count):
        count = counts_ref[0, doc]
        tally = jnp.where((row >= start) & (row < start + count), count, tally)
        slots = jnp.where((lane >= start) & (lane < start + count), slots_ref[first_doc + doc], slots)
        start = start + count
    leader = (lax.axis_index("cuts") == 0).astype(jnp.float32)
    payload_ref[row_count:, :] = slots.astype(jnp.float32) * leader
    copies[2].wait()
    copies[3].wait()
    outward = lax.dot_general(grads_ref[...], out_ref[...], contract, preferred_element_type=jnp.float32)
    payload_ref[:row_count, rank:] = outward / tally.astype(jnp.float32)
    copies[0].wait()
    copies[1].wait()
    inward = lax.dot_general(acts_ref[...], in_ref[...], contract, preferred_element_type=jnp.float32)
    payload_ref[:row_count, :rank] = inward


def project(counts, doc_slots, activations, out_grads, proj_in, proj_out):
    row_count, rank = activations.shape[0], proj_in.shape[1]
    operands = (activations, proj_in.T, out_grads, proj_out.T, counts, doc_slots)
    spaces = [pltpu.VMEM] * 4 + [pltpu.SMEM] * 2
    return pl.pallas_call(
        project_kernel,
        in_specs=[pl.BlockSpec(memory_space=pltpu.HBM)] * len(operands),
        out_specs=pl.BlockSpec(memory_space=pltpu.VMEM),
        scratch_shapes=[space(operand.shape, operand.dtype) for space, operand in zip(spaces, operands)]
        + [pltpu.SemaphoreType.DMA((len(operands),))],
        out_shape=jax.ShapeDtypeStruct((row_count + TILE, 2 * rank), jnp.float32),
        compiler_params=pltpu.CompilerParams(vmem_limit_bytes=60 * 1024 * 1024),
        name="project",
    )(*operands)


def score_kernel(row_count, rank, origins, other, payload_ref, query_ref, scores_ref, outward_ref):
    sources = payload_ref.shape[0]
    query_rows, columns = scores_ref.shape
    chunks, halves = query_ref.shape[:2]
    split = query_ref.shape[3] // rank
    tokens = sources * row_count
    here = lax.axis_index("dp") * lax.axis_size("cuts") + lax.axis_index("cuts")
    parts = lax.axis_size("dp") * lax.axis_size("cuts")
    half = here // (parts // halves)
    target = halves - 1 - half if other else half
    payload = payload_ref[...]
    turned = payload[:, :row_count, :].reshape(tokens, 2 * rank).T
    inward = turned[:rank]
    outward_ref[...] = turned[rank:]
    high = inward.astype(jnp.bfloat16)
    low = (inward - high.astype(jnp.float32)).astype(jnp.bfloat16)
    blank = jnp.zeros_like(high)
    group = math.gcd(split, max(1, LANES // rank))
    total = jnp.zeros((query_rows, tokens), jnp.float32)
    for part in range(split):
        first = part // group * group
        query = query_ref[:, target, :, first * rank:(first + group) * rank].reshape(chunks * query_rows, group * rank)
        column = [blank] * (2 * group)
        column[part - first], column[part - first + group] = high, low
        met = jnp.dot(
            jnp.concatenate([query, query], axis=1),
            jnp.concatenate(column, axis=0),
            preferred_element_type=jnp.float32,
        )
        for chunk in range(chunks):
            origin = half * chunks + chunk if origins is None else here ^ origins[chunk]
            factor = outward_ref[pl.ds(origin * split + part, 1), :]
            total = total + met[chunk * query_rows:(chunk + 1) * query_rows] * factor
    marks = payload[:, row_count:, :].reshape(sources * TILE, 2 * rank).T
    slots = jnp.concatenate([marks[:row_count, s * TILE:s * TILE + 1] for s in range(sources)], axis=0)
    column_of = lax.broadcasted_iota(jnp.int32, (tokens, columns), 1)
    member = (slots.astype(jnp.int32) == column_of).astype(jnp.bfloat16)
    total_high = total.astype(jnp.bfloat16)
    total_low = (total - total_high.astype(jnp.float32)).astype(jnp.bfloat16)
    scores = jnp.dot(total_high, member, preferred_element_type=jnp.float32)
    scores = scores + jnp.dot(total_low, member, preferred_element_type=jnp.float32)

    @pl.when(pl.program_id(0) == 0)
    def _():
        scores_ref[...] = scores

    @pl.when(pl.program_id(0) > 0)
    def _():
        scores_ref[...] += scores


def score(payload, query, columns, row_count, rank, origins, other):
    sources = payload.shape[0]
    query_rows = query.shape[2]
    step = min(sources, 8)
    return pl.pallas_call(
        functools.partial(score_kernel, row_count, rank, origins, other),
        grid=(sources // step,),
        in_specs=[
            pl.BlockSpec((step,) + payload.shape[1:], lambda i: (i, 0, 0)),
            pl.BlockSpec(query.shape, lambda i: (0, 0, 0, 0)),
        ],
        out_specs=pl.BlockSpec((query_rows, columns), lambda i: (0, 0)),
        out_shape=jax.ShapeDtypeStruct((query_rows, columns), jnp.float32),
        scratch_shapes=[pltpu.VMEM((rank, step * row_count), jnp.float32)],
        compiler_params=pltpu.CompilerParams(vmem_limit_bytes=48 * 1024 * 1024),
        name="score_other" if other else "score_own",
    )(payload, query)


def exchange(value, axis, bit):
    count = lax.axis_size(axis)
    return lax.ppermute(value, axis, [(i, i ^ bit) for i in range(count)])


def pick(value, index, axis):
    return lax.dynamic_index_in_dim(value, index, axis, keepdims=False)


def on_device(activations, out_grads, counts, doc_slots, proj_in, proj_out, queries):
    row_count = activations.shape[0]
    rank = proj_in.shape[1]
    both = ("dp", "cuts")
    cut_count = lax.axis_size("cuts")
    parts = cut_count * lax.axis_size("dp")
    query_rows = queries.shape[0] // parts
    width = queries.shape[1]

    flip = cut_count - 1
    here = lax.axis_index(both)
    half = here // (parts // 2)
    bits = [1 << place for place in range((parts // 2 - 1).bit_length())]
    order = [bit for bit in bits if bit >= cut_count] + [bit for bit in bits if bit < cut_count]
    waiting = bits[::-1]
    arrived = queries.reshape([1, 2] + [2] * len(bits) + [query_rows, width])
    origins = [0]
    for bit in order:
        place = 1 + waiting.index(bit)
        waiting.remove(bit)
        own = (here // bit) % 2
        if bit >= cut_count:
            leaving, staying = pick(arrived, 1 - own, place + 1), pick(arrived, own, place + 1)
        else:
            sides = [jnp.where(half == top, own, 1 - own) for top in range(2)]
            leaving = jnp.stack([pick(arrived[:, top], 1 - sides[top], place) for top in range(2)], axis=1)
            staying = jnp.stack([pick(arrived[:, top], sides[top], place) for top in range(2)], axis=1)
        landed = exchange(leaving, both, bit)
        if width % rank:
            pair = (jnp.where(own == 0, staying, landed), jnp.where(own == 0, landed, staying))
            arrived = jnp.stack(pair, axis=1).reshape((-1,) + staying.shape[1:])
        else:
            arrived = jnp.concatenate([staying, landed], axis=0)
        origins = origins + [origin ^ bit for origin in origins]
    arrived = arrived.reshape(parts // 2, 2, query_rows, width)
    if width % rank:
        arrived = arrived.reshape([2] * len(bits) + [2, query_rows, width])
        axes = [order.index(bit) for bit in bits[::-1]]
        arrived = arrived.transpose([len(bits), len(bits) + 1] + axes + [len(bits) + 2])
        arrived = arrived.reshape(2, query_rows, -1, rank).transpose(2, 0, 1, 3)
        origins = None

    payload = project(counts, doc_slots, activations, out_grads, proj_in, proj_out)
    bit = 1
    while bit < cut_count:
        payload = payload + exchange(payload, "cuts", bit)
        bit *= 2
    payload = payload[None]
    far = [bit for bit in bits + [parts // 2] if bit >= cut_count]
    for bit in far[-2:] + far[-3::-1]:
        payload = jnp.concatenate([payload, exchange(payload, both, bit ^ flip)], axis=0)
    columns = doc_slots.shape[0]
    theirs = score(payload, arrived, columns, row_count, rank, origins, True)
    own = score(payload, arrived, columns, row_count, rank, origins, False)
    return own + exchange(theirs, both, parts // 2 ^ flip)


def solution(mesh):
    placed = (
        P(("groups", "dp"), "cuts"),
        P(("groups", "dp"), "cuts"),
        P(("groups", "dp"), None),
        P("groups"),
        P("cuts", None),
        P("cuts", None),
        P(None, ("dp", "cuts")),
    )
    return jax.shard_map(
        on_device,
        mesh=mesh,
        in_specs=placed,
        out_specs=P(("dp", "cuts"), "groups"),
        check_vma=False,
    )
```

```python
import functools
import math

import jax
import jax.numpy as jnp
from jax import lax
from jax.experimental import pallas as pl
from jax.experimental.pallas import tpu as pltpu
from jax.sharding import PartitionSpec as P

TILE = 8
LANES = 128


def project_kernel(*refs):
    sources, payload_ref, held, sem = refs[:6], refs[6], refs[7:13], refs[13]
    copies = [pltpu.make_async_copy(source, kept, sem.at[i]) for i, (source, kept) in enumerate(zip(sources, held))]
    for i in (4, 5, 2, 3, 0, 1):
        copies[i].start()
    acts_ref, in_ref, grads_ref, out_ref, counts_ref, slots_ref = held
    row_count = acts_ref.shape[0]
    rank = in_ref.shape[0]
    doc_count = counts_ref.shape[1]
    contract = (((1,), (1,)), ((), ()))
    row = lax.broadcasted_iota(jnp.int32, (row_count, rank), 0)
    lane = lax.broadcasted_iota(jnp.int32, (TILE, 2 * rank), 1)
    tally = jnp.ones((row_count, rank), jnp.int32)
    slots = jnp.zeros((TILE, 2 * rank), jnp.int32)
    first_doc = lax.axis_index("dp") * doc_count
    copies[4].wait()
    copies[5].wait()
    start = jnp.int32(0)
    for doc in range(doc_count):
        count = counts_ref[0, doc]
        tally = jnp.where((row >= start) & (row < start + count), count, tally)
        slots = jnp.where((lane >= start) & (lane < start + count), slots_ref[first_doc + doc], slots)
        start = start + count
    leader = (lax.axis_index("cuts") == 0).astype(jnp.float32)
    payload_ref[row_count:, :] = slots.astype(jnp.float32) * leader
    copies[2].wait()
    copies[3].wait()
    outward = lax.dot_general(grads_ref[...], out_ref[...], contract, preferred_element_type=jnp.float32)
    payload_ref[:row_count, rank:] = outward / tally.astype(jnp.float32)
    copies[0].wait()
    copies[1].wait()
    inward = lax.dot_general(acts_ref[...], in_ref[...], contract, preferred_element_type=jnp.float32)
    payload_ref[:row_count, :rank] = inward


def project(counts, doc_slots, activations, out_grads, proj_in, proj_out):
    row_count, rank = activations.shape[0], proj_in.shape[1]
    operands = (activations, proj_in.T, out_grads, proj_out.T, counts, doc_slots)
    spaces = [pltpu.VMEM] * 4 + [pltpu.SMEM] * 2
    return pl.pallas_call(
        project_kernel,
        in_specs=[pl.BlockSpec(memory_space=pltpu.HBM)] * len(operands),
        out_specs=pl.BlockSpec(memory_space=pltpu.VMEM),
        scratch_shapes=[space(operand.shape, operand.dtype) for space, operand in zip(spaces, operands)]
        + [pltpu.SemaphoreType.DMA((len(operands),))],
        out_shape=jax.ShapeDtypeStruct((row_count + TILE, 2 * rank), jnp.float32),
        compiler_params=pltpu.CompilerParams(vmem_limit_bytes=60 * 1024 * 1024),
        name="project",
    )(*operands)


def score_kernel(row_count, rank, origins, other, *refs):
    payload_ref, query_ref = refs[:2]
    base_ref = refs[2] if len(refs) == 5 else None
    scores_ref, outward_ref = refs[-2:]
    sources = payload_ref.shape[0]
    query_rows, columns = scores_ref.shape
    chunks, halves = query_ref.shape[:2]
    split = query_ref.shape[3] // rank
    tokens = sources * row_count
    here = lax.axis_index("dp") * lax.axis_size("cuts") + lax.axis_index("cuts")
    parts = lax.axis_size("dp") * lax.axis_size("cuts")
    half = here // (parts // halves)
    target = halves - 1 - half if other else half
    payload = payload_ref[...]
    turned = payload[:, :row_count, :].reshape(tokens, 2 * rank).T
    inward = turned[:rank]
    outward_ref[...] = turned[rank:]
    high = inward.astype(jnp.bfloat16)
    low = (inward - high.astype(jnp.float32)).astype(jnp.bfloat16)
    blank = jnp.zeros_like(high)
    group = math.gcd(split, max(1, LANES // rank))
    total = jnp.zeros((query_rows, tokens), jnp.float32)
    for part in range(split):
        first = part // group * group
        query = query_ref[:, target, :, first * rank:(first + group) * rank].reshape(chunks * query_rows, group * rank)
        column = [blank] * (2 * group)
        column[part - first], column[part - first + group] = high, low
        met = jnp.dot(
            jnp.concatenate([query, query], axis=1),
            jnp.concatenate(column, axis=0),
            preferred_element_type=jnp.float32,
        )
        for chunk in range(chunks):
            origin = half * chunks + chunk if origins is None else here ^ origins[chunk]
            factor = outward_ref[pl.ds(origin * split + part, 1), :]
            total = total + met[chunk * query_rows:(chunk + 1) * query_rows] * factor
    marks = payload[:, row_count:, :].reshape(sources * TILE, 2 * rank).T
    slots = jnp.concatenate([marks[:row_count, s * TILE:s * TILE + 1] for s in range(sources)], axis=0)
    column_of = lax.broadcasted_iota(jnp.int32, (tokens, columns), 1)
    member = (slots.astype(jnp.int32) == column_of).astype(jnp.bfloat16)
    total_high = total.astype(jnp.bfloat16)
    total_low = (total - total_high.astype(jnp.float32)).astype(jnp.bfloat16)
    scores = jnp.dot(total_high, member, preferred_element_type=jnp.float32)
    scores = scores + jnp.dot(total_low, member, preferred_element_type=jnp.float32)

    @pl.when(pl.program_id(0) == 0)
    def _():
        scores_ref[...] = scores if base_ref is None else scores + base_ref[...]

    @pl.when(pl.program_id(0) > 0)
    def _():
        scores_ref[...] += scores


def score(payload, query, columns, row_count, rank, origins, other, base=None):
    sources = payload.shape[0]
    query_rows = query.shape[2]
    step = min(sources, 8)
    return pl.pallas_call(
        functools.partial(score_kernel, row_count, rank, origins, other),
        grid=(sources // step,),
        in_specs=[
            pl.BlockSpec((step,) + payload.shape[1:], lambda i: (i, 0, 0)),
            pl.BlockSpec(query.shape, lambda i: (0, 0, 0, 0)),
        ]
        + [pl.BlockSpec((query_rows, columns), lambda i: (0, 0))] * (base is not None),
        out_specs=pl.BlockSpec((query_rows, columns), lambda i: (0, 0)),
        out_shape=jax.ShapeDtypeStruct((query_rows, columns), jnp.float32),
        scratch_shapes=[pltpu.VMEM((rank, step * row_count), jnp.float32)],
        compiler_params=pltpu.CompilerParams(vmem_limit_bytes=48 * 1024 * 1024),
        name="score_other" if other else "score_own",
    )(payload, query, *([] if base is None else [base]))


def exchange(value, axis, bit):
    count = lax.axis_size(axis)
    return lax.ppermute(value, axis, [(i, i ^ bit) for i in range(count)])


def pick(value, index, axis):
    return lax.dynamic_index_in_dim(value, index, axis, keepdims=False)


def on_device(activations, out_grads, counts, doc_slots, proj_in, proj_out, queries):
    row_count = activations.shape[0]
    rank = proj_in.shape[1]
    both = ("dp", "cuts")
    cut_count = lax.axis_size("cuts")
    parts = cut_count * lax.axis_size("dp")
    query_rows = queries.shape[0] // parts
    width = queries.shape[1]

    flip = cut_count - 1
    here = lax.axis_index(both)
    half = here // (parts // 2)
    bits = [1 << place for place in range((parts // 2 - 1).bit_length())]
    order = bits
    waiting = bits[::-1]
    arrived = queries.reshape([1, 2] + [2] * len(bits) + [query_rows, width])
    origins = [0]
    for bit in order:
        place = 1 + waiting.index(bit)
        waiting.remove(bit)
        own = (here // bit) % 2
        if bit >= cut_count:
            leaving, staying = pick(arrived, 1 - own, place + 1), pick(arrived, own, place + 1)
        else:
            sides = [jnp.where(half == top, own, 1 - own) for top in range(2)]
            leaving = jnp.stack([pick(arrived[:, top], 1 - sides[top], place) for top in range(2)], axis=1)
            staying = jnp.stack([pick(arrived[:, top], sides[top], place) for top in range(2)], axis=1)
        landed = exchange(leaving, both, bit)
        if width % rank:
            pair = (jnp.where(own == 0, staying, landed), jnp.where(own == 0, landed, staying))
            arrived = jnp.stack(pair, axis=1).reshape((-1,) + staying.shape[1:])
        else:
            arrived = jnp.concatenate([staying, landed], axis=0)
        origins = origins + [origin ^ bit for origin in origins]
    arrived = arrived.reshape(parts // 2, 2, query_rows, width)
    if width % rank:
        arrived = arrived.reshape([2] * len(bits) + [2, query_rows, width])
        axes = [order.index(bit) for bit in bits[::-1]]
        arrived = arrived.transpose([len(bits), len(bits) + 1] + axes + [len(bits) + 2])
        arrived = arrived.reshape(2, query_rows, -1, rank).transpose(2, 0, 1, 3)
        origins = None

    payload = project(counts, doc_slots, activations, out_grads, proj_in, proj_out)
    bit = 1
    while bit < cut_count:
        payload = payload + exchange(payload, "cuts", bit)
        bit *= 2
    payload = payload[None]
    far = [bit for bit in bits + [parts // 2] if bit >= cut_count]
    *early, last = far[-2:] + far[-3::-1]
    for bit in early:
        payload = jnp.concatenate([payload, exchange(payload, both, bit ^ flip)], axis=0)
    landed = exchange(payload, both, last ^ flip)
    columns = doc_slots.shape[0]
    sizes = (columns, row_count, rank, origins)
    theirs = score(payload, arrived, *sizes, True)
    theirs = score(landed, arrived, *sizes, True, theirs)
    own = score(payload, arrived, *sizes, False)
    own = score(landed, arrived, *sizes, False, own)
    return own + exchange(theirs, both, parts // 2 ^ flip)


def solution(mesh):
    placed = (
        P(("groups", "dp"), "cuts"),
        P(("groups", "dp"), "cuts"),
        P(("groups", "dp"), None),
        P("groups"),
        P("cuts", None),
        P("cuts", None),
        P(None, ("dp", "cuts")),
    )
    return jax.shard_map(
        on_device,
        mesh=mesh,
        in_specs=placed,
        out_specs=P(("dp", "cuts"), "groups"),
        check_vma=False,
    )
```

```python
import functools
import math

import jax
import jax.numpy as jnp
from jax import lax
from jax.experimental import pallas as pl
from jax.experimental.pallas import tpu as pltpu
from jax.sharding import PartitionSpec as P

TILE = 8
LANES = 128


def project_kernel(*refs):
    sources, payload_ref, held, sem = refs[:6], refs[6], refs[7:13], refs[13]
    copies = [pltpu.make_async_copy(source, kept, sem.at[i]) for i, (source, kept) in enumerate(zip(sources, held))]
    for i in (4, 5, 2, 3, 0, 1):
        copies[i].start()
    acts_ref, in_ref, grads_ref, out_ref, counts_ref, slots_ref = held
    row_count = acts_ref.shape[0]
    rank = in_ref.shape[0]
    doc_count = counts_ref.shape[1]
    contract = (((1,), (1,)), ((), ()))
    row = lax.broadcasted_iota(jnp.int32, (row_count, rank), 0)
    lane = lax.broadcasted_iota(jnp.int32, (TILE, 2 * rank), 1)
    tally = jnp.ones((row_count, rank), jnp.int32)
    slots = jnp.zeros((TILE, 2 * rank), jnp.int32)
    first_doc = lax.axis_index("dp") * doc_count
    copies[4].wait()
    copies[5].wait()
    start = jnp.int32(0)
    for doc in range(doc_count):
        count = counts_ref[0, doc]
        tally = jnp.where((row >= start) & (row < start + count), count, tally)
        slots = jnp.where((lane >= start) & (lane < start + count), slots_ref[first_doc + doc], slots)
        start = start + count
    leader = (lax.axis_index("cuts") == 0).astype(jnp.float32)
    payload_ref[row_count:, :] = slots.astype(jnp.float32) * leader
    copies[2].wait()
    copies[3].wait()
    outward = lax.dot_general(grads_ref[...], out_ref[...], contract, preferred_element_type=jnp.float32)
    payload_ref[:row_count, rank:] = outward / tally.astype(jnp.float32)
    copies[0].wait()
    copies[1].wait()
    inward = lax.dot_general(acts_ref[...], in_ref[...], contract, preferred_element_type=jnp.float32)
    payload_ref[:row_count, :rank] = inward


def project(counts, doc_slots, activations, out_grads, proj_in, proj_out):
    row_count, rank = activations.shape[0], proj_in.shape[1]
    operands = (activations, proj_in.T, out_grads, proj_out.T, counts, doc_slots)
    spaces = [pltpu.VMEM] * 4 + [pltpu.SMEM] * 2
    return pl.pallas_call(
        project_kernel,
        in_specs=[pl.BlockSpec(memory_space=pltpu.HBM)] * len(operands),
        out_specs=pl.BlockSpec(memory_space=pltpu.VMEM),
        scratch_shapes=[space(operand.shape, operand.dtype) for space, operand in zip(spaces, operands)]
        + [pltpu.SemaphoreType.DMA((len(operands),))],
        out_shape=jax.ShapeDtypeStruct((row_count + TILE, 2 * rank), jnp.float32),
        compiler_params=pltpu.CompilerParams(vmem_limit_bytes=60 * 1024 * 1024),
        name="project",
    )(*operands)


def score_kernel(row_count, rank, origins, other, *refs):
    payload_ref, query_ref = refs[:2]
    base_ref = refs[2] if len(refs) == 5 else None
    scores_ref, outward_ref = refs[-2:]
    sources = payload_ref.shape[0]
    query_rows, columns = scores_ref.shape
    chunks, halves = query_ref.shape[:2]
    split = query_ref.shape[3] // rank
    tokens = sources * row_count
    here = lax.axis_index("dp") * lax.axis_size("cuts") + lax.axis_index("cuts")
    parts = lax.axis_size("dp") * lax.axis_size("cuts")
    half = here // (parts // halves)
    target = halves - 1 - half if other else half
    payload = payload_ref[...]
    turned = payload[:, :row_count, :].reshape(tokens, 2 * rank).T
    inward = turned[:rank]
    outward_ref[...] = turned[rank:]
    high = inward.astype(jnp.bfloat16)
    low = (inward - high.astype(jnp.float32)).astype(jnp.bfloat16)
    blank = jnp.zeros_like(high)
    group = math.gcd(split, max(1, LANES // rank))
    total = jnp.zeros((query_rows, tokens), jnp.float32)
    for part in range(split):
        first = part // group * group
        query = query_ref[:, target, :, first * rank:(first + group) * rank].reshape(chunks * query_rows, group * rank)
        column = [blank] * (2 * group)
        column[part - first], column[part - first + group] = high, low
        met = jnp.dot(
            jnp.concatenate([query, query], axis=1),
            jnp.concatenate(column, axis=0),
            preferred_element_type=jnp.float32,
        )
        for chunk in range(chunks):
            origin = half * chunks + chunk if origins is None else here ^ origins[chunk]
            factor = outward_ref[pl.ds(origin * split + part, 1), :]
            total = total + met[chunk * query_rows:(chunk + 1) * query_rows] * factor
    marks = payload[:, row_count:, :].reshape(sources * TILE, 2 * rank).T
    slots = jnp.concatenate([marks[:row_count, s * TILE:s * TILE + 1] for s in range(sources)], axis=0)
    column_of = lax.broadcasted_iota(jnp.int32, (tokens, columns), 1)
    member = (slots.astype(jnp.int32) == column_of).astype(jnp.bfloat16)
    total_high = total.astype(jnp.bfloat16)
    total_low = (total - total_high.astype(jnp.float32)).astype(jnp.bfloat16)
    scores = jnp.dot(total_high, member, preferred_element_type=jnp.float32)
    scores = scores + jnp.dot(total_low, member, preferred_element_type=jnp.float32)

    @pl.when(pl.program_id(0) == 0)
    def _():
        scores_ref[...] = scores if base_ref is None else scores + base_ref[...]

    @pl.when(pl.program_id(0) > 0)
    def _():
        scores_ref[...] += scores


def score(payload, query, columns, row_count, rank, origins, other, base=None):
    sources = payload.shape[0]
    query_rows = query.shape[2]
    step = min(sources, 8)
    return pl.pallas_call(
        functools.partial(score_kernel, row_count, rank, origins, other),
        grid=(sources // step,),
        in_specs=[
            pl.BlockSpec((step,) + payload.shape[1:], lambda i: (i, 0, 0)),
            pl.BlockSpec(query.shape, lambda i: (0, 0, 0, 0)),
        ]
        + [pl.BlockSpec((query_rows, columns), lambda i: (0, 0))] * (base is not None),
        out_specs=pl.BlockSpec((query_rows, columns), lambda i: (0, 0)),
        out_shape=jax.ShapeDtypeStruct((query_rows, columns), jnp.float32),
        scratch_shapes=[pltpu.VMEM((rank, step * row_count), jnp.float32)],
        compiler_params=pltpu.CompilerParams(vmem_limit_bytes=48 * 1024 * 1024),
        name="score_other" if other else "score_own",
    )(payload, query, *([] if base is None else [base]))


def exchange(value, axis, bit):
    count = lax.axis_size(axis)
    return lax.ppermute(value, axis, [(i, i ^ bit) for i in range(count)])


def pick(value, index, axis):
    return lax.dynamic_index_in_dim(value, index, axis, keepdims=False)


def on_device(activations, out_grads, counts, doc_slots, proj_in, proj_out, queries):
    row_count = activations.shape[0]
    rank = proj_in.shape[1]
    both = ("dp", "cuts")
    cut_count = lax.axis_size("cuts")
    parts = cut_count * lax.axis_size("dp")
    query_rows = queries.shape[0] // parts
    width = queries.shape[1]

    flip = cut_count - 1
    here = lax.axis_index(both)
    half = here // (parts // 2)
    bits = [1 << place for place in range((parts // 2 - 1).bit_length())]
    order = bits
    waiting = bits[::-1]
    arrived = queries.reshape([1, 2] + [2] * len(bits) + [query_rows, width])
    origins = [0]
    for bit in order:
        place = 1 + waiting.index(bit)
        waiting.remove(bit)
        own = (here // bit) % 2
        if bit >= cut_count:
            leaving, staying = pick(arrived, 1 - own, place + 1), pick(arrived, own, place + 1)
        else:
            sides = [jnp.where(half == top, own, 1 - own) for top in range(2)]
            leaving = jnp.stack([pick(arrived[:, top], 1 - sides[top], place) for top in range(2)], axis=1)
            staying = jnp.stack([pick(arrived[:, top], sides[top], place) for top in range(2)], axis=1)
        landed = exchange(leaving, both, bit)
        if width % rank:
            pair = (jnp.where(own == 0, staying, landed), jnp.where(own == 0, landed, staying))
            arrived = jnp.stack(pair, axis=1).reshape((-1,) + staying.shape[1:])
        else:
            arrived = jnp.concatenate([staying, landed], axis=0)
        origins = origins + [origin ^ bit for origin in origins]
    arrived = arrived.reshape(parts // 2, 2, query_rows, width)
    if width % rank:
        arrived = arrived.reshape([2] * len(bits) + [2, query_rows, width])
        axes = [order.index(bit) for bit in bits[::-1]]
        arrived = arrived.transpose([len(bits), len(bits) + 1] + axes + [len(bits) + 2])
        arrived = arrived.reshape(2, query_rows, -1, rank).transpose(2, 0, 1, 3)
        origins = None

    payload = project(counts, doc_slots, activations, out_grads, proj_in, proj_out)
    bit = 1
    while bit < cut_count:
        payload = payload + exchange(payload, "cuts", bit)
        bit *= 2
    payload = payload[None]
    far = [bit for bit in bits + [parts // 2] if bit >= cut_count]
    *early, last = far[-2:] + far[-3::-1]
    for bit in early:
        payload = jnp.concatenate([payload, exchange(payload, both, bit ^ flip)], axis=0)
    landed = exchange(payload, both, last)
    columns = doc_slots.shape[0]
    sizes = (columns, row_count, rank, origins)
    theirs = score(payload, arrived, *sizes, True)
    theirs = score(landed, arrived, *sizes, True, theirs)
    own = score(payload, arrived, *sizes, False)
    own = score(landed, arrived, *sizes, False, own)
    return own + exchange(theirs, both, parts // 2 ^ flip)


def solution(mesh):
    placed = (
        P(("groups", "dp"), "cuts"),
        P(("groups", "dp"), "cuts"),
        P(("groups", "dp"), None),
        P("groups"),
        P("cuts", None),
        P("cuts", None),
        P(None, ("dp", "cuts")),
    )
    return jax.shard_map(
        on_device,
        mesh=mesh,
        in_specs=placed,
        out_specs=P(("dp", "cuts"), "groups"),
        check_vma=False,
    )
```
